32 devices in a mesh: pb: 8 (over y, x, core), ka: 4 (over z).
Axes of the slice: x: 2, y: 2, z: 4, core: 2. Of those that a mesh axis runs over, the one named last changes fastest.
Arguments:
- first_layer_query: bfloat16 [4096, 4096], P(('pb', 'ka')), may hold values from -8 to 8
- second_layer_query: bfloat16 [4096, 4096], P(('pb', 'ka')), may hold values from -8 to 8
- shared_keys: bfloat16 [4096, 512], P(('pb', 'ka')), may hold values from -8 to 8
- shared_values: bfloat16 [4096, 512], P(('pb', 'ka')), may hold values from -6 to 6
- block_mask: int32 [32, 32], P(('pb', 'ka')), may hold values 0 or 1
- doc_lengths: int32 [32], replicated, may hold values from 1 to 256, 4096 in all
Outputs:
- attended_first: bfloat16 [4096, 4096], P(('pb', 'ka'))
- attended_second: bfloat16 [4096, 4096], P(('pb', 'ka'))
The draws below stay inside these ranges and needn't reach their ends.
Inputs may be any that keep to these rules, and one draw needn't show every extreme that they name: `doc_lengths`: document lengths in packing order; they sum to 4096, and one document is exactly 256 long.
All inputs are finite; a program needn't handle non-finite values. No bound on the sum of `block_mask` on one device may be relied on, other than what follows from the above.
Results may differ from the reference program's by a relative error of at most 0.004.
Values may be sent and summed in bfloat16 or wider, within the bound.
A program may use at most 64 MiB of HBM per device.

```python
import math
import jax
import jax.numpy as jnp
import numpy as np
from jax import lax

QUERY_HEADS = 32
SHARED_KV_HEADS = 4
HEAD_SIZE = 128
BLK = 128
TOK_DEV = 128
CONTEXT_TOKENS = 4096
DOC_MAX = 256
NDOC = 32
NB = 32
N_KA = 4


def drawn_query(key, random_salt):
    base_offset = jax.random.normal(jax.random.fold_in(key, random_salt), (CONTEXT_TOKENS, QUERY_HEADS * HEAD_SIZE))
    return jnp.clip(base_offset, -6.0, 6.0).astype(jnp.bfloat16)


def draw_first_layer_query(key, part):
    return drawn_query(key, 1)


def draw_second_layer_query(key, part):
    return drawn_query(key, 2)


def draw_shared_keys(key, part):
    base_offset = jax.random.normal(jax.random.fold_in(key, 3), (CONTEXT_TOKENS, SHARED_KV_HEADS * HEAD_SIZE))
    return jnp.clip(base_offset, -6.0, 6.0).astype(jnp.bfloat16)


def with_ends(values, stream_key, least, top_value):
    place = [jax.random.randint(jax.random.fold_in(stream_key, axis), (), 0, length) for axis, length in enumerate(values.shape)]
    longest = values.shape.index(max(values.shape))
    neighbour = place[:longest] + [(place[longest] + 1) % values.shape[longest]] + place[longest + 1:]
    return values.at[tuple(place)].set(least).at[tuple(neighbour)].set(top_value)


def block_scale(rng, shape, cuts, least, high):
    loudness = 1.0
    for dim, blocks in cuts:
        draws = jax.random.uniform(jax.random.fold_in(jax.random.fold_in(rng, 6), dim), (blocks,), jnp.float32, least / len(cuts), high / len(cuts))
        loudness = loudness * jnp.repeat(jnp.exp(draws), shape[dim] // blocks).reshape((-1,) + (1,) * (len(shape) - 1 - dim))
    return loudness


def split_up(count, total, most, skew):
    weights = [(1 << 20) // math.isqrt(grade ** skew) + 1 for grade in range(2, count + 1)]
    rest, given = total - most - (count - 1), [1] * (count - 1)
    while rest > 0:
        candidates = [i for i in range(count - 1) if given[i] < most]
        whole, remaining = sum([weights[i] for i in candidates]), rest
        for i in candidates:
            more = min(most - given[i], max(1, remaining * weights[i] // whole), rest)
            given[i] = given[i] + more
            rest = rest - more
    return np.array([most] + given)


def ragged(stream_key, count, total, bound, skew):
    if count == 2:
        one = jax.random.randint(stream_key, (), max(1, total - bound), min(bound, total - 1) + 1)
        return jnp.stack([one, total - one])
    tallies = jnp.asarray(split_up(count, total, bound, skew), jnp.int32)
    couples = (count - 1) // 2
    giver, taker = tallies[1:1 + 2 * couples:2], tallies[2:2 + 2 * couples:2]
    slack = jnp.minimum(giver - 1, bound - taker)
    moved = jax.random.randint(jax.random.fold_in(stream_key, 1), (couples,), 0, 1 << 20) % (slack + 1)
    tallies = tallies.at[1:1 + 2 * couples:2].set(giver - moved).at[2:2 + 2 * couples:2].set(taker + moved)
    return tallies[jax.random.permutation(jax.random.fold_in(stream_key, 2), count)]


def normal_values(key, extent, deviation, reach, cuts=(), kind=jnp.bfloat16):
    gain = block_scale(key, extent, cuts, -0.22, 0.18) if cuts else 1.0
    drawn = jax.random.normal(key, extent, jnp.float32) * deviation * gain
    return jnp.minimum(jnp.maximum(drawn, -reach), reach).astype(kind)


def setup_inputs(seed: int = 0) -> dict:
    seeds = jax.random.split(jax.random.key(seed), 7)
    return {
        "first_layer_query": draw_first_layer_query(jax.random.fold_in(seeds[6], 71), 0),
        "second_layer_query": draw_second_layer_query(jax.random.fold_in(seeds[6], 71), 0),
        "shared_keys": draw_shared_keys(jax.random.fold_in(seeds[6], 71), 0),
        "shared_values": normal_values(seeds[3], (CONTEXT_TOKENS, SHARED_KV_HEADS * HEAD_SIZE), 1.0, 6.0, ((0, 32),)),
        "block_mask": with_ends((jax.random.randint(seeds[4], (NB, NB), 0, 4) < 3).astype(jnp.int32), jax.random.fold_in(seeds[4], 1), 0, 1),
        "doc_lengths": ragged(seeds[5], NDOC, CONTEXT_TOKENS, DOC_MAX, 0).astype(jnp.int32),
    }


def reference(first_layer_query, second_layer_query, shared_keys, shared_values, block_mask, doc_lengths):
    token_matrix = TOK_DEV
    span_steps = N_KA // 2 + 1
    window_span = span_steps * token_matrix
    query_groups = QUERY_HEADS // SHARED_KV_HEADS
    block_rows = token_matrix // BLK
    score_scale = 1.0 / math.sqrt(HEAD_SIZE)
    padded_keys = jnp.concatenate([jnp.zeros((window_span - token_matrix, SHARED_KV_HEADS * HEAD_SIZE), shared_keys.dtype), shared_keys], axis=0)
    padded_values = jnp.concatenate([jnp.zeros((window_span - token_matrix, SHARED_KV_HEADS * HEAD_SIZE), shared_values.dtype), shared_values], axis=0)
    stacked = jnp.stack([first_layer_query, second_layer_query])
    starts = jnp.cumsum(doc_lengths) - doc_lengths

    def doc_of(position):
        return lax.optimization_barrier(jnp.sum((starts[None, :] <= position[:, None]).astype(jnp.int32), axis=1)) - 1

    def one_stretch(span_index):
        query_rows = lax.dynamic_slice_in_dim(stacked, span_index * token_matrix, token_matrix, 1)
        query_rows = query_rows.reshape(2, token_matrix, SHARED_KV_HEADS, query_groups, HEAD_SIZE).astype(jnp.float32)
        key_head_rows = lax.dynamic_slice_in_dim(padded_keys, span_index * token_matrix, window_span, 0).reshape(window_span, SHARED_KV_HEADS, HEAD_SIZE).astype(jnp.float32)
        value_head_rows = lax.dynamic_slice_in_dim(padded_values, span_index * token_matrix, window_span, 0).reshape(window_span, SHARED_KV_HEADS, HEAD_SIZE).astype(jnp.float32)
        query_pos = span_index * token_matrix + jnp.arange(token_matrix, dtype=jnp.int32)
        key_pos = (span_index - span_steps + 1) * token_matrix + jnp.arange(window_span, dtype=jnp.int32)
        mask_rows = lax.dynamic_slice_in_dim(block_mask, span_index * block_rows, block_rows, 0)
        local_block = query_pos // BLK - span_index * block_rows
        key_block = jnp.clip(key_pos // BLK, 0, NB - 1)
        picked = jnp.take(jnp.take(mask_rows, local_block, axis=0), key_block, axis=1) == 1
        same_block = key_pos[None, :] // BLK == query_pos[:, None] // BLK
        allowed = (key_pos[None, :] >= 0) & (key_pos[None, :] <= query_pos[:, None])
        allowed = allowed & (doc_of(key_pos)[None, :] == doc_of(query_pos)[:, None]) & (picked | same_block)
        scores = jnp.einsum('lqkgd,tkd->lkgqt', query_rows, key_head_rows) * score_scale
        masked = jnp.where(allowed, scores, -1e+30)
        top = lax.optimization_barrier(jnp.max(masked, axis=-1))
        weights = jnp.where(allowed, jnp.exp(masked - top[..., None]), 0.0)
        total = lax.optimization_barrier(jnp.sum(weights, axis=-1))
        rounded = weights.astype(jnp.bfloat16).astype(jnp.float32)
        summed = jnp.einsum('lkgqt,tkd->lkgqd', rounded, value_head_rows)
        result = summed / total[..., None]
        result = jnp.transpose(result, (0, 3, 1, 2, 4)).reshape(2, token_matrix, QUERY_HEADS * HEAD_SIZE)
        return result.astype(jnp.bfloat16)
    outputs = lax.map(one_stretch, jnp.arange(CONTEXT_TOKENS // token_matrix, dtype=jnp.int32))
    outputs = jnp.transpose(outputs, (1, 0, 2, 3)).reshape(2, CONTEXT_TOKENS, QUERY_HEADS * HEAD_SIZE)
    return (outputs[0], outputs[1])
```

```python
import functools
import math

import jax
import jax.numpy as jnp
from jax import lax
from jax.experimental import pallas as pl
from jax.experimental.pallas import tpu as pltpu
from jax.sharding import PartitionSpec as P

QUERY_HEADS = 32
SHARED_KV_HEADS = 4
HEAD_SIZE = 128
BLK = 128
STACK = 2
MESH = pl.DeviceIdType.MESH
ROWS_BY_LANES = (((1,), (1,)), ((), ()))


def kernel(
    groups, ka, far, docs, mask_ref, q0_hbm, q1_hbm, k_hbm, v_hbm, out0, out1,
    kv, qbuf, bias, part, top, load_sem, q_sem, send_sem, cross_sem, recv_sem,
):
    tokens = k_hbm.shape[0]
    heads = SHARED_KV_HEADS
    per = QUERY_HEADS // heads
    pb = lax.axis_index("pb")
    z = lax.axis_index("ka")
    span = pb * ka + z
    queries = (q0_hbm, q1_hbm)
    outs = (out0, out1)

    gets_up = z >= 1
    gets_cross = (z == 0) & (pb >= 1)
    sends_up = z + 1 < ka
    sends_cross = (z >= ka - far) & (pb + 1 < groups)
    above = (pb, jnp.minimum(z + 1, ka - 1))
    after = (jnp.minimum(pb + 1, groups - 1), 0)

    def when(cond, *acts):
        @pl.when(cond)
        def _():
            for act in acts:
                act()

    barrier = pltpu.get_barrier_semaphore()

    def greet(cond, device):
        when(cond, lambda: pl.semaphore_signal(
            barrier, inc=1, device_id=device, device_id_type=MESH))

    for j in range(1, far + 1):
        greet(gets_cross, (jnp.maximum(pb - 1, 0), ka - j))
    greet(gets_up, (pb, jnp.maximum(z - 1, 0)))

    def columns(g):
        return pl.ds(g * HEAD_SIZE, HEAD_SIZE)

    def loads(g):
        return (
            pltpu.make_async_copy(k_hbm.at[:, columns(g)], kv.at[g, 0, 0], load_sem.at[0, g]),
            pltpu.make_async_copy(v_hbm.at[:, columns(g)], kv.at[g, 0, 1], load_sem.at[1, g]),
        )

    def query_loads(g):
        return [
            pltpu.make_async_copy(
                queries[l].at[:, pl.ds(g * per * HEAD_SIZE, per * HEAD_SIZE)],
                qbuf.at[g, l], q_sem.at[l, g],
            )
            for l in range(2)
        ]

    for g in range(heads):
        for copy in loads(g):
            copy.start()
    for g in range(heads):
        for copy in query_loads(g):
            copy.start()

    def remote(j, g, to, device, sem):
        return pltpu.make_async_remote_copy(
            src_ref=kv.at[g, j],
            dst_ref=kv.at[g, to],
            send_sem=sem,
            recv_sem=recv_sem.at[to, g],
            device_id=device,
            device_id_type=MESH,
        )

    def cross(g):
        return remote(0, g, jnp.minimum(ka - z, far), after, cross_sem.at[g])

    def up(j, g):
        return remote(j, g, j + 1, above, send_sem.at[j, g])

    def here(j):
        return (z >= j) | (pb >= 1)

    def take(j, g):
        when(here(j), lambda: remote(j, g, j, (pb, z), recv_sem.at[j, g]).wait_recv())

    peers = sends_up.astype(jnp.int32) + sends_cross.astype(jnp.int32)
    when(peers >= 1, lambda: pl.semaphore_wait(barrier, peers))

    for g in range(heads):
        for copy in loads(g):
            copy.wait()
        when(sends_up, lambda: up(0, g).start())
        when(sends_cross, lambda: cross(g).start())

    for j in range(1, far + 1):

        @pl.when(jnp.logical_not(here(j)))
        def _():
            kv[:, j] = jnp.zeros(kv.shape[:1] + kv.shape[2:], kv.dtype)

    row = lax.broadcasted_iota(jnp.int32, (tokens, tokens), 0) + span * tokens
    lane = lax.broadcasted_iota(jnp.int32, (tokens, tokens), 1)

    def next_doc(d, carry):
        begin, first = carry
        first = jnp.where(row >= begin, begin, first)
        return begin + docs[d], first

    _, first = lax.fori_loop(
        0, docs.shape[0], next_doc, (jnp.int32(0), jnp.zeros((tokens, tokens), jnp.int32))
    )
    for j in range(far + 1):
        key = lane + (span - j) * tokens
        ok = (key >= first) & (key <= row)
        if j > 0:
            open_block = jnp.full((tokens, tokens), mask_ref[0, jnp.maximum(span - j, 0)])
            ok = ok & (open_block == 1)
        bias[:, pl.ds(j * tokens, tokens)] = jnp.where(ok, 0.0, -1e30)

    factor = math.log2(math.e) / math.sqrt(HEAD_SIZE)
    near = far * tokens

    def score(g, l, h, k, off):
        q = qbuf[g, l, :, pl.ds(h * HEAD_SIZE, HEAD_SIZE)]
        s = lax.dot_general(q, k, ROWS_BY_LANES, preferred_element_type=jnp.float32)
        return s * factor + bias[:, pl.ds(off, k.shape[0])]

    def weigh(w, v):
        both = jnp.concatenate([v, jnp.ones_like(v)], axis=1)
        return jnp.dot(w.astype(jnp.bfloat16), both, preferred_element_type=jnp.float32)

    def begin(g, l, h):
        k = kv[g, :far, 0].reshape(near, HEAD_SIZE)
        v = kv[g, :far, 1].reshape(near, HEAD_SIZE)
        s = score(g, l, h, k, 0)
        m = jnp.max(s, axis=1, keepdims=True)
        part[g, l, h] = weigh(jnp.exp2(s - m), v)
        top[g, l, h] = jnp.broadcast_to(m, (tokens, HEAD_SIZE))

    def finish(g, l, h):
        s = score(g, l, h, kv[g, far, 0], near)
        old = top[g, l, h]
        m = jnp.maximum(old, jnp.max(s, axis=1, keepdims=True))
        o = weigh(jnp.exp2(s - m), kv[g, far, 1])
        shrink = jnp.exp2(old - m)
        value = part[g, l, h, :, :HEAD_SIZE] * shrink + o[:, :HEAD_SIZE]
        total = part[g, l, h, :, HEAD_SIZE:] * shrink + o[:, HEAD_SIZE:]
        outs[l][:, pl.ds((g * per + h) * HEAD_SIZE, HEAD_SIZE)] = (value / total).astype(jnp.bfloat16)

    for g in range(heads):
        for j in range(1, far):
            take(j, g)
            when(sends_up & here(j), lambda: up(j, g).start())
        for copy in query_loads(g):
            copy.wait()
        for l in range(2):
            for h in range(per):
                begin(g, l, h)
    for g in range(heads):
        take(far, g)
        for l in range(2):
            for h in range(per):
                finish(g, l, h)

    for g in range(heads):
        when(sends_cross, lambda: cross(g).wait_send())
        for j in range(far):
            when(sends_up & here(j), lambda: up(j, g).wait_send())


def write_out(first, second, o0_hbm, o1_hbm, sem):
    copies = [
        pltpu.make_async_copy(first, o0_hbm, sem.at[0]),
        pltpu.make_async_copy(second, o1_hbm, sem.at[1]),
    ]
    for copy in copies:
        copy.start()
    for copy in copies:
        copy.wait()


def solution(mesh):
    groups, ka = mesh.shape["pb"], mesh.shape["ka"]
    far = ka // 2

    def shards(q0, q1, k, v, block_mask, doc_lengths):
        tokens, width = q0.shape
        heads = SHARED_KV_HEADS
        per = QUERY_HEADS // heads
        assert tokens == BLK and block_mask.shape[0] == 1
        out = jax.ShapeDtypeStruct((tokens, width), jnp.bfloat16)
        held = pltpu.VMEM((tokens, width), jnp.bfloat16)
        smem = pl.BlockSpec(memory_space=pltpu.SMEM)
        vmem = pl.BlockSpec(memory_space=pltpu.VMEM)
        hbm = pl.BlockSpec(memory_space=pl.ANY)
        first, second = pl.pallas_call(
            functools.partial(kernel, groups, ka, far),
            out_shape=(held, held),
            in_specs=[smem, smem] + [hbm] * 4,
            out_specs=(vmem, vmem),
            scratch_shapes=[
                pltpu.VMEM((heads, far + 1, 2, tokens, HEAD_SIZE), jnp.bfloat16),
                pltpu.VMEM((heads, 2, tokens, width // heads), jnp.bfloat16),
                pltpu.VMEM((tokens, (far + 1) * tokens), jnp.float32),
                pltpu.VMEM((heads, 2, per, tokens, 2 * HEAD_SIZE), jnp.float32),
                pltpu.VMEM((heads, 2, per, tokens, HEAD_SIZE), jnp.float32),
                pltpu.SemaphoreType.DMA((2, heads)),
                pltpu.SemaphoreType.DMA((2, heads)),
                pltpu.SemaphoreType.DMA((far, heads)),
                pltpu.SemaphoreType.DMA((heads,)),
                pltpu.SemaphoreType.DMA((far + 1, heads)),
            ],
            compiler_params=pltpu.CompilerParams(
                collective_id=0, has_side_effects=True, vmem_limit_bytes=60 * 2**20
            ),
        )(doc_lengths, block_mask, q0, q1, k, v)
        first = pltpu.with_memory_space_constraint(first, pltpu.VMEM)
        second = pltpu.with_memory_space_constraint(second, pltpu.VMEM)
        return pl.pallas_call(
            write_out,
            out_shape=(out, out),
            in_specs=[vmem, vmem],
            out_specs=(hbm, hbm),
            scratch_shapes=[pltpu.SemaphoreType.DMA((2,))],
        )(first, second)

    split = P(("pb", "ka"), None)
    return jax.shard_map(
        shards, mesh=mesh, in_specs=(split,) * 5 + (P(),), out_specs=(split, split), check_vma=False
    )
```

```python
import functools
import math

import jax
import jax.numpy as jnp
from jax import lax
from jax.experimental import pallas as pl
from jax.experimental.pallas import tpu as pltpu
from jax.sharding import PartitionSpec as P

QUERY_HEADS = 32
SHARED_KV_HEADS = 4
HEAD_SIZE = 128
BLK = 128
STACK = 8
MESH = pl.DeviceIdType.MESH
ROWS_BY_LANES = (((1,), (1,)), ((), ()))


def kernel(
    groups, ka, far, docs, mask_ref, q0_hbm, q1_hbm, k_hbm, v_hbm,
    lead0, lead1, late_part, late_weight, late_value,
    kv, hop, qbuf, bias, part, top, load_sem, q_sem, send_sem, cross_sem, recv_sem,
    hop_send_sem, hop_recv_sem,
):
    tokens = k_hbm.shape[0]
    heads = SHARED_KV_HEADS
    per = QUERY_HEADS // heads
    last = heads - 1
    pb = lax.axis_index("pb")
    z = lax.axis_index("ka")
    span = pb * ka + z
    queries = (q0_hbm, q1_hbm)
    own = (k_hbm, v_hbm)
    leads = (lead0, lead1)

    def shifted(group):
        count = heads * (group // 2 + 1) // max(groups // 2, 1)
        return jnp.where((group % 2 == 1) & (group + 1 < groups), count, 0)

    gets_up = z >= 1
    gets_cross = (z == 0) & (pb >= 1)
    sends_up = z + 1 < ka
    ends = z >= ka - far
    sends_cross = ends & (pb + 1 < groups)
    moves_out = jnp.where(sends_cross, shifted(pb), 0)
    moves_in = jnp.where(pb >= 1, shifted(pb - 1), 0)
    moves_on = jnp.where(ends, moves_in, 0)
    above = (pb, jnp.minimum(z + 1, ka - 1))
    below = (pb, jnp.maximum(z - 1, 0))
    beside = (jnp.minimum(pb + 1, groups - 1), z)
    after = (jnp.minimum(pb + 1, groups - 1), 0)
    before = jnp.maximum(pb - 1, 0)

    def when(cond, *acts):
        @pl.when(cond)
        def _():
            for act in acts:
                act()

    barrier = pltpu.get_barrier_semaphore()

    def greet(cond, device):
        when(cond, lambda: pl.semaphore_signal(
            barrier, inc=1, device_id=device, device_id_type=MESH))

    for j in range(1, far + 1):
        greet(gets_cross, (before, ka - j))
    greet(gets_up, below)
    for j in range(1, far + 1):
        greet((z == 0) & (moves_in >= 1), (pb, ka - j))
    greet(moves_on >= 1, (before, z))

    def columns(g):
        return pl.ds(g * HEAD_SIZE, HEAD_SIZE)

    def loads(g):
        return [
            pltpu.make_async_copy(own[p].at[:, columns(g)], kv.at[g, 0, p], load_sem.at[p, g])
            for p in range(2)
        ]

    def query_loads(g):
        return [
            pltpu.make_async_copy(
                queries[l].at[:, pl.ds(g * per * HEAD_SIZE, per * HEAD_SIZE)],
                qbuf.at[g, l], q_sem.at[l, g],
            )
            for l in range(2)
        ]

    for g in range(heads):
        for copy in loads(g):
            copy.start()
    for g in range(heads):
        for copy in query_loads(g):
            copy.start()

    def parts(g):
        return range(2) if g == last else range(1)

    def place(ref, g, p):
        return ref.at[p] if g == last else ref

    def remote(src, dst, g, p, device, send, recv):
        return pltpu.make_async_remote_copy(
            src_ref=place(src, g, p),
            dst_ref=place(dst, g, p),
            send_sem=send.at[g, p],
            recv_sem=recv.at[g, p],
            device_id=device,
            device_id_type=MESH,
        )

    slot = jnp.clip(ka - z, 1, far)

    def cross(g, p):
        return remote(
            kv.at[g, 0], kv.at[g, slot], g, p, after, cross_sem, recv_sem.at[slot])

    def move(g, p):
        return remote(kv.at[g, 0], hop.at[g], g, p, beside, cross_sem, hop_recv_sem)

    def pass_on(g, p):
        return remote(hop.at[g], kv.at[g, slot], g, p, (pb, 0), hop_send_sem, recv_sem.at[slot])

    def up(j, g, p):
        return remote(
            kv.at[g, j], kv.at[g, j + 1], g, p, above, send_sem.at[j], recv_sem.at[j + 1])

    def here(j):
        return (z >= j) | (pb >= 1)

    def take(j, g, p):
        when(here(j), lambda: remote(
            kv.at[g, j], kv.at[g, j], g, p, (pb, z), cross_sem, recv_sem.at[j]).wait_recv())

    def hand_on(g):
        @pl.when(moves_on > last - g)
        def _():
            for p in parts(g):
                move(g, p).wait_recv()
                pass_on(g, p).start()

    peers = (
        sends_up.astype(jnp.int32) + sends_cross.astype(jnp.int32)
        + (moves_out >= 1).astype(jnp.int32) + (moves_on >= 1).astype(jnp.int32)
    )
    when(peers >= 1, lambda: pl.semaphore_wait(barrier, peers))

    for g in range(heads):
        for copy in loads(g):
            copy.wait()
    for g in range(heads):
        for p in parts(g):
            when(moves_out > last - g, lambda: move(g, p).start())
    for g in range(heads):
        for p in parts(g):
            when(sends_up, lambda: up(0, g, p).start())
        for p in parts(g):
            when(sends_cross & (moves_out <= last - g), lambda: cross(g, p).start())

    for j in range(1, far + 1):

        @pl.when(jnp.logical_not(here(j)))
        def _():
            kv[:, j] = jnp.zeros(kv.shape[:1] + kv.shape[2:], kv.dtype)

    row = lax.broadcasted_iota(jnp.int32, (tokens, tokens), 0) + span * tokens
    lane = lax.broadcasted_iota(jnp.int32, (tokens, tokens), 1)

    def next_doc(d, carry):
        begin, first = carry
        first = jnp.where(row >= begin, begin, first)
        return begin + docs[d], first

    _, first = lax.fori_loop(
        0, docs.shape[0], next_doc, (jnp.int32(0), jnp.zeros((tokens, tokens), jnp.int32))
    )
    for j in range(far + 1):
        key = lane + (span - j) * tokens
        ok = (key >= first) & (key <= row)
        if j > 0:
            open_block = jnp.full((tokens, tokens), mask_ref[0, jnp.maximum(span - j, 0)])
            ok = ok & (open_block == 1)
        bias[:, pl.ds(j * tokens, tokens)] = jnp.where(ok, 0.0, -1e30)

    factor = math.log2(math.e) / math.sqrt(HEAD_SIZE)
    near = far * tokens

    rows = STACK * tokens

    def score(g, l, h, k, off):
        q = jnp.concatenate(
            [qbuf[g, l, :, pl.ds((h + i) * HEAD_SIZE, HEAD_SIZE)] for i in range(STACK)], axis=0)
        s = lax.dot_general(q, k, ROWS_BY_LANES, preferred_element_type=jnp.float32)
        mask = bias[:, pl.ds(off, k.shape[0])]
        return s * factor + jnp.concatenate([mask] * STACK, axis=0)

    def begin(g, l, h):
        k = kv[g, :far, 0].reshape(near, HEAD_SIZE)
        v = kv[g, :far, 1].reshape(near, HEAD_SIZE)
        s = score(g, l, h, k, 0)
        m = jnp.max(s, axis=1, keepdims=True)
        o = weigh(jnp.exp2(s - m).astype(jnp.bfloat16), v)
        part[g, l, pl.ds(h, STACK)] = o.reshape(STACK, tokens, 2 * HEAD_SIZE)
        top[g, l, pl.ds(h, STACK)] = jnp.broadcast_to(m, (rows, HEAD_SIZE)).reshape(
            STACK, tokens, HEAD_SIZE)

    def fold(g, l, h):
        s = score(g, l, h, kv[g, far, 0], near)
        old = top[g, l, pl.ds(h, STACK)].reshape(rows, HEAD_SIZE)
        m = jnp.maximum(old, jnp.max(s, axis=1, keepdims=True))
        shrink = jnp.exp2(old - m)
        w = jnp.exp2(s - m).astype(jnp.bfloat16)
        rest = part[g, l, pl.ds(h, STACK)].reshape(rows, 2 * HEAD_SIZE)
        return w, rest * jnp.concatenate([shrink, shrink], axis=1)

    def finish(g, l, h):
        w, rest = fold(g, l, h)
        o = ratio(rest + weigh(w, kv[g, far, 1]))
        for i in range(STACK):
            leads[l][:, pl.ds((g * per + h + i) * HEAD_SIZE, HEAD_SIZE)] = (
                o[i * tokens : (i + 1) * tokens])

    def prepare(g, l, h):
        w, rest = fold(g, l, h)
        late_weight[l, pl.ds(h, STACK)] = w.reshape(STACK, tokens, HEAD_SIZE)
        late_part[l, pl.ds(h, STACK)] = rest.reshape(STACK, tokens, 2 * HEAD_SIZE)

    def every(act, g):
        for l in range(2):
            for h in range(0, per, STACK):
                act(g, l, h)

    def end(g, cond):
        @pl.when(cond)
        def _():
            for p in parts(g):
                take(far, g, p)
            every(finish, g)

    for g in range(1, heads):
        hand_on(g)
    def receive(g):
        for j in range(1, far):
            for p in parts(g):
                take(j, g, p)
                when(sends_up & here(j), lambda: up(j, g, p).start())

    receive(0)
    for g in range(heads):
        for copy in query_loads(g):
            copy.wait()
        every(begin, g)
        if g < last:
            receive(g + 1)
    for g in range(last):
        for p in parts(g):
            take(far, g, p)
        every(finish, g)
    take(far, last, 0)
    every(prepare, last)
    take(far, last, 1)
    late_value[...] = kv[last, far, 1]

    for g in range(heads):
        for p in parts(g):
            when(sends_cross, lambda: cross(g, p).wait_send())
            when(moves_on > last - g, lambda: pass_on(g, p).wait_send())
            for j in range(far):
                when(sends_up & here(j), lambda: up(j, g, p).wait_send())


def weigh(w, v):
    both = jnp.concatenate([v, jnp.ones_like(v)], axis=1)
    return jnp.dot(w, both, preferred_element_type=jnp.float32)


def ratio(o):
    return (o[:, :HEAD_SIZE] / o[:, HEAD_SIZE:]).astype(jnp.bfloat16)


def write_out(lead0, lead1, late_part, late_weight, late_value, out0, out1, late, lead_sem, late_sem):
    wide = lead0.shape[1]
    rest = out0.shape[1] - wide
    leads, outs = (lead0, lead1), (out0, out1)
    copies = [
        pltpu.make_async_copy(leads[l], outs[l].at[:, pl.ds(0, wide)], lead_sem.at[l])
        for l in range(2)
    ]
    for copy in copies:
        copy.start()
    for l in range(2):
        for h in range(late_part.shape[1]):
            late[l, :, pl.ds(h * HEAD_SIZE, HEAD_SIZE)] = ratio(
                late_part[l, h] + weigh(late_weight[l, h], late_value[...]))
        copy = pltpu.make_async_copy(late.at[l], outs[l].at[:, pl.ds(wide, rest)], late_sem.at[l])
        copy.start()
        copies.append(copy)
    for copy in copies:
        copy.wait()


def solution(mesh):
    groups, ka = mesh.shape["pb"], mesh.shape["ka"]
    far = ka // 2

    def shards(q0, q1, k, v, block_mask, doc_lengths):
        tokens, width = q0.shape
        heads = SHARED_KV_HEADS
        per = QUERY_HEADS // heads
        assert tokens == BLK and block_mask.shape[0] == 1
        out = jax.ShapeDtypeStruct((tokens, width), jnp.bfloat16)
        lead = pltpu.VMEM((tokens, width - width // heads), jnp.bfloat16)
        held = (
            lead, lead,
            pltpu.VMEM((2, per, tokens, 2 * HEAD_SIZE), jnp.float32),
            pltpu.VMEM((2, per, tokens, HEAD_SIZE), jnp.bfloat16),
            pltpu.VMEM((tokens, HEAD_SIZE), jnp.bfloat16),
        )
        smem = pl.BlockSpec(memory_space=pltpu.SMEM)
        vmem = pl.BlockSpec(memory_space=pltpu.VMEM)
        hbm = pl.BlockSpec(memory_space=pl.ANY)
        results = pl.pallas_call(
            functools.partial(kernel, groups, ka, far),
            out_shape=held,
            in_specs=[smem, smem] + [hbm] * 4,
            out_specs=(vmem,) * len(held),
            scratch_shapes=[
                pltpu.VMEM((heads, far + 1, 2, tokens, HEAD_SIZE), jnp.bfloat16),
                pltpu.VMEM((heads, 2, tokens, HEAD_SIZE), jnp.bfloat16),
                pltpu.VMEM((heads, 2, tokens, width // heads), jnp.bfloat16),
                pltpu.VMEM((tokens, (far + 1) * tokens), jnp.float32),
                pltpu.VMEM((heads, 2, per, tokens, 2 * HEAD_SIZE), jnp.float32),
                pltpu.VMEM((heads, 2, per, tokens, HEAD_SIZE), jnp.float32),
                pltpu.SemaphoreType.DMA((2, heads)),
                pltpu.SemaphoreType.DMA((2, heads)),
                pltpu.SemaphoreType.DMA((far, heads, 2)),
                pltpu.SemaphoreType.DMA((heads, 2)),
                pltpu.SemaphoreType.DMA((far + 1, heads, 2)),
                pltpu.SemaphoreType.DMA((heads, 2)),
                pltpu.SemaphoreType.DMA((heads, 2)),
            ],
            compiler_params=pltpu.CompilerParams(
                collective_id=0, has_side_effects=True, vmem_limit_bytes=56 * 2**20
            ),
        )(doc_lengths, block_mask, q0, q1, k, v)
        results = [pltpu.with_memory_space_constraint(x, pltpu.VMEM) for x in results]
        return pl.pallas_call(
            write_out,
            out_shape=(out, out),
            in_specs=[vmem] * len(held),
            out_specs=(hbm, hbm),
            scratch_shapes=[
                pltpu.VMEM((2, tokens, width // heads), jnp.bfloat16),
                pltpu.SemaphoreType.DMA((2,)),
                pltpu.SemaphoreType.DMA((2,)),
            ],
            compiler_params=pltpu.CompilerParams(vmem_limit_bytes=16 * 2**20),
        )(*results)

    split = P(("pb", "ka"), None)
    return jax.shard_map(
        shards, mesh=mesh, in_specs=(split,) * 5 + (P(),), out_specs=(split, split), check_vma=False
    )
```

```python
import functools
import math

import jax
import jax.numpy as jnp
from jax import lax
from jax.experimental import pallas as pl
from jax.experimental.pallas import tpu as pltpu
from jax.sharding import PartitionSpec as P

QUERY_HEADS = 32
SHARED_KV_HEADS = 4
HEAD_SIZE = 128
BLK = 128
STACK = 8
MESH = pl.DeviceIdType.MESH
ROWS_BY_LANES = (((1,), (1,)), ((), ()))


def kernel(
    groups, ka, far, docs, mask_ref, q0_hbm, q1_hbm, k_hbm, v_hbm,
    lead0, lead1, late_part, late_weight, late_value,
    kv, hop, qbuf, bias, part, top, load_sem, q_sem, send_sem, cross_sem, recv_sem,
    hop_send_sem, hop_recv_sem,
):
    tokens = k_hbm.shape[0]
    heads = SHARED_KV_HEADS
    per = QUERY_HEADS // heads
    last = heads - 1
    pb = lax.axis_index("pb")
    z = lax.axis_index("ka")
    span = pb * ka + z
    queries = (q0_hbm, q1_hbm)
    own = (k_hbm, v_hbm)
    leads = (lead0, lead1)

    def shifted(group, at):
        chips = max(groups // 2, 1)
        count = heads * (chips // 2 + group // 2 + 1) // chips
        return jnp.where((group % 2 == 1) & (group + 1 < groups), (count + (ka - at) % 2) // 2, 0)

    gets_up = z >= 1
    gets_cross = (z == 0) & (pb >= 1)
    sends_up = z + 1 < ka
    ends = z >= ka - far
    sends_cross = ends & (pb + 1 < groups)
    moves_out = jnp.where(sends_cross, shifted(pb, z), 0)
    moves_on = jnp.where(ends & (pb >= 1), shifted(pb - 1, z), 0)
    above = (pb, jnp.minimum(z + 1, ka - 1))
    below = (pb, jnp.maximum(z - 1, 0))
    beside = (jnp.minimum(pb + 1, groups - 1), z)
    after = (jnp.minimum(pb + 1, groups - 1), 0)
    before = jnp.maximum(pb - 1, 0)

    def when(cond, *acts):
        @pl.when(cond)
        def _():
            for act in acts:
                act()

    barrier = pltpu.get_barrier_semaphore()

    def greet(cond, device):
        when(cond, lambda: pl.semaphore_signal(
            barrier, inc=1, device_id=device, device_id_type=MESH))

    for j in range(1, far + 1):
        greet(gets_cross, (before, ka - j))
    greet(gets_up, below)
    for j in range(1, far + 1):
        greet(gets_cross & (shifted(pb - 1, ka - j) >= 1), (pb, ka - j))
    greet(moves_on >= 1, (before, z))

    def columns(g):
        return pl.ds(g * HEAD_SIZE, HEAD_SIZE)

    def loads(g):
        return [
            pltpu.make_async_copy(own[p].at[:, columns(g)], kv.at[g, 0, p], load_sem.at[p, g])
            for p in range(2)
        ]

    def query_loads(g):
        return [
            pltpu.make_async_copy(
                queries[l].at[:, pl.ds(g * per * HEAD_SIZE, per * HEAD_SIZE)],
                qbuf.at[g, l], q_sem.at[l, g],
            )
            for l in range(2)
        ]

    for g in range(heads):
        for copy in loads(g):
            copy.start()
    for g in range(heads):
        for copy in query_loads(g):
            copy.start()

    def parts(g):
        return range(2) if g == last else range(1)

    def place(ref, g, p):
        return ref.at[p] if g == last else ref

    def remote(src, dst, g, p, device, send, recv):
        return pltpu.make_async_remote_copy(
            src_ref=place(src, g, p),
            dst_ref=place(dst, g, p),
            send_sem=send.at[g, p],
            recv_sem=recv.at[g, p],
            device_id=device,
            device_id_type=MESH,
        )

    slot = jnp.clip(ka - z, 1, far)

    def cross(g, p):
        return remote(
            kv.at[g, 0], kv.at[g, slot], g, p, after, cross_sem, recv_sem.at[slot])

    def move(g, p):
        return remote(kv.at[g, 0], hop.at[g], g, p, beside, cross_sem, hop_recv_sem)

    def pass_on(g, p):
        return remote(hop.at[g], kv.at[g, slot], g, p, (pb, 0), hop_send_sem, recv_sem.at[slot])

    def up(j, g, p):
        return remote(
            kv.at[g, j], kv.at[g, j + 1], g, p, above, send_sem.at[j], recv_sem.at[j + 1])

    def here(j):
        return (z >= j) | (pb >= 1)

    def take(j, g, p):
        when(here(j), lambda: remote(
            kv.at[g, j], kv.at[g, j], g, p, (pb, z), cross_sem, recv_sem.at[j]).wait_recv())

    def hand_on(g):
        @pl.when(moves_on > last - g)
        def _():
            for p in parts(g):
                move(g, p).wait_recv()
                pass_on(g, p).start()

    peers = (
        sends_up.astype(jnp.int32) + sends_cross.astype(jnp.int32)
        + (moves_out >= 1).astype(jnp.int32) + (moves_on >= 1).astype(jnp.int32)
    )
    when(peers >= 1, lambda: pl.semaphore_wait(barrier, peers))

    for g in range(heads):
        for copy in loads(g):
            copy.wait()
    for g in range(heads):
        for p in parts(g):
            when(moves_out > last - g, lambda: move(g, p).start())
    for g in range(heads):
        for p in parts(g):
            when(sends_up, lambda: up(0, g, p).start())
        for p in parts(g):
            when(sends_cross & (moves_out <= last - g), lambda: cross(g, p).start())

    for j in range(1, far + 1):

        @pl.when(jnp.logical_not(here(j)))
        def _():
            kv[:, j] = jnp.zeros(kv.shape[:1] + kv.shape[2:], kv.dtype)

    row = lax.broadcasted_iota(jnp.int32, (tokens, tokens), 0) + span * tokens
    lane = lax.broadcasted_iota(jnp.int32, (tokens, tokens), 1)

    def next_doc(d, carry):
        begin, first = carry
        first = jnp.where(row >= begin, begin, first)
        return begin + docs[d], first

    _, first = lax.fori_loop(
        0, docs.shape[0], next_doc, (jnp.int32(0), jnp.zeros((tokens, tokens), jnp.int32))
    )
    for j in range(far + 1):
        key = lane + (span - j) * tokens
        ok = (key >= first) & (key <= row)
        if j > 0:
            open_block = jnp.full((tokens, tokens), mask_ref[0, jnp.maximum(span - j, 0)])
            ok = ok & (open_block == 1)
        bias[:, pl.ds(j * tokens, tokens)] = jnp.where(ok, 0.0, -1e30)

    factor = math.log2(math.e) / math.sqrt(HEAD_SIZE)
    near = far * tokens

    rows = STACK * tokens

    def score(g, l, h, k, off):
        q = jnp.concatenate(
            [qbuf[g, l, :, pl.ds((h + i) * HEAD_SIZE, HEAD_SIZE)] for i in range(STACK)], axis=0)
        s = lax.dot_general(q, k, ROWS_BY_LANES, preferred_element_type=jnp.float32)
        mask = bias[:, pl.ds(off, k.shape[0])]
        return s * factor + jnp.concatenate([mask] * STACK, axis=0)

    def begin(g, l, h):
        k = kv[g, :far, 0].reshape(near, HEAD_SIZE)
        v = kv[g, :far, 1].reshape(near, HEAD_SIZE)
        s = score(g, l, h, k, 0)
        m = jnp.max(s, axis=1, keepdims=True)
        o = weigh(jnp.exp2(s - m).astype(jnp.bfloat16), v)
        part[g, l, pl.ds(h, STACK)] = o.reshape(STACK, tokens, 2 * HEAD_SIZE)
        top[g, l, pl.ds(h, STACK)] = jnp.broadcast_to(m, (rows, HEAD_SIZE)).reshape(
            STACK, tokens, HEAD_SIZE)

    def fold(g, l, h):
        s = score(g, l, h, kv[g, far, 0], near)
        old = top[g, l, pl.ds(h, STACK)].reshape(rows, HEAD_SIZE)
        m = jnp.maximum(old, jnp.max(s, axis=1, keepdims=True))
        shrink = jnp.exp2(old - m)
        w = jnp.exp2(s - m).astype(jnp.bfloat16)
        rest = part[g, l, pl.ds(h, STACK)].reshape(rows, 2 * HEAD_SIZE)
        return w, rest * jnp.concatenate([shrink, shrink], axis=1)

    def finish(g, l, h):
        w, rest = fold(g, l, h)
        o = ratio(rest + weigh(w, kv[g, far, 1]))
        for i in range(STACK):
            leads[l][:, pl.ds((g * per + h + i) * HEAD_SIZE, HEAD_SIZE)] = (
                o[i * tokens : (i + 1) * tokens])

    def prepare(g, l, h):
        w, rest = fold(g, l, h)
        late_weight[l, pl.ds(h, STACK)] = w.reshape(STACK, tokens, HEAD_SIZE)
        late_part[l, pl.ds(h, STACK)] = rest.reshape(STACK, tokens, 2 * HEAD_SIZE)

    def every(act, g):
        for l in range(2):
            for h in range(0, per, STACK):
                act(g, l, h)

    for g in range(1, heads):
        hand_on(g)
    def receive(g):
        for j in range(1, far):
            for p in parts(g):
                take(j, g, p)
                when(sends_up & here(j), lambda: up(j, g, p).start())

    receive(0)
    for g in range(heads):
        for copy in query_loads(g):
            copy.wait()
        every(begin, g)
        if g < last:
            receive(g + 1)
    for g in range(last):
        for p in parts(g):
            take(far, g, p)
        every(finish, g)
    take(far, last, 0)
    every(prepare, last)
    take(far, last, 1)
    late_value[...] = kv[last, far, 1]

    for g in range(heads):
        for p in parts(g):
            when(sends_cross, lambda: cross(g, p).wait_send())
            when(moves_on > last - g, lambda: pass_on(g, p).wait_send())
            for j in range(far):
                when(sends_up & here(j), lambda: up(j, g, p).wait_send())


def weigh(w, v):
    both = jnp.concatenate([v, jnp.ones_like(v)], axis=1)
    return jnp.dot(w, both, preferred_element_type=jnp.float32)


def ratio(o):
    return (o[:, :HEAD_SIZE] / o[:, HEAD_SIZE:]).astype(jnp.bfloat16)


def write_out(lead0, lead1, late_part, late_weight, late_value, out0, out1, late, lead_sem, late_sem):
    wide = lead0.shape[1]
    rest = out0.shape[1] - wide
    leads, outs = (lead0, lead1), (out0, out1)
    copies = [
        pltpu.make_async_copy(leads[l], outs[l].at[:, pl.ds(0, wide)], lead_sem.at[l])
        for l in range(2)
    ]
    for copy in copies:
        copy.start()
    for l in range(2):
        for h in range(late_part.shape[1]):
            late[l, :, pl.ds(h * HEAD_SIZE, HEAD_SIZE)] = ratio(
                late_part[l, h] + weigh(late_weight[l, h], late_value[...]))
        copy = pltpu.make_async_copy(late.at[l], outs[l].at[:, pl.ds(wide, rest)], late_sem.at[l])
        copy.start()
        copies.append(copy)
    for copy in copies:
        copy.wait()


def solution(mesh):
    groups, ka = mesh.shape["pb"], mesh.shape["ka"]
    far = ka // 2

    def shards(q0, q1, k, v, block_mask, doc_lengths):
        tokens, width = q0.shape
        heads = SHARED_KV_HEADS
        per = QUERY_HEADS // heads
        assert tokens == BLK and block_mask.shape[0] == 1
        out = jax.ShapeDtypeStruct((tokens, width), jnp.bfloat16)
        lead = pltpu.VMEM((tokens, width - width // heads), jnp.bfloat16)
        held = (
            lead, lead,
            pltpu.VMEM((2, per, tokens, 2 * HEAD_SIZE), jnp.float32),
            pltpu.VMEM((2, per, tokens, HEAD_SIZE), jnp.bfloat16),
            pltpu.VMEM((tokens, HEAD_SIZE), jnp.bfloat16),
        )
        smem = pl.BlockSpec(memory_space=pltpu.SMEM)
        vmem = pl.BlockSpec(memory_space=pltpu.VMEM)
        hbm = pl.BlockSpec(memory_space=pl.ANY)
        results = pl.pallas_call(
            functools.partial(kernel, groups, ka, far),
            out_shape=held,
            in_specs=[smem, smem] + [hbm] * 4,
            out_specs=(vmem,) * len(held),
            scratch_shapes=[
                pltpu.VMEM((heads, far + 1, 2, tokens, HEAD_SIZE), jnp.bfloat16),
                pltpu.VMEM((heads, 2, tokens, HEAD_SIZE), jnp.bfloat16),
                pltpu.VMEM((heads, 2, tokens, width // heads), jnp.bfloat16),
                pltpu.VMEM((tokens, (far + 1) * tokens), jnp.float32),
                pltpu.VMEM((heads, 2, per, tokens, 2 * HEAD_SIZE), jnp.float32),
                pltpu.VMEM((heads, 2, per, tokens, HEAD_SIZE), jnp.float32),
                pltpu.SemaphoreType.DMA((2, heads)),
                pltpu.SemaphoreType.DMA((2, heads)),
                pltpu.SemaphoreType.DMA((far, heads, 2)),
                pltpu.SemaphoreType.DMA((heads, 2)),
                pltpu.SemaphoreType.DMA((far + 1, heads, 2)),
                pltpu.SemaphoreType.DMA((heads, 2)),
                pltpu.SemaphoreType.DMA((heads, 2)),
            ],
            compiler_params=pltpu.CompilerParams(
                collective_id=0, has_side_effects=True, vmem_limit_bytes=56 * 2**20
            ),
        )(doc_lengths, block_mask, q0, q1, k, v)
        results = [pltpu.with_memory_space_constraint(x, pltpu.VMEM) for x in results]
        return pl.pallas_call(
            write_out,
            out_shape=(out, out),
            in_specs=[vmem] * len(held),
            out_specs=(hbm, hbm),
            scratch_shapes=[
                pltpu.VMEM((2, tokens, width // heads), jnp.bfloat16),
                pltpu.SemaphoreType.DMA((2,)),
                pltpu.SemaphoreType.DMA((2,)),
            ],
            compiler_params=pltpu.CompilerParams(vmem_limit_bytes=16 * 2**20),
        )(*results)

    split = P(("pb", "ka"), None)
    return jax.shard_map(
        shards, mesh=mesh, in_specs=(split,) * 5 + (P(),), out_specs=(split, split), check_vma=False
    )
```
